512 devices in a mesh: dp: 128 (over z, y, core), mp: 4 (over x).
Axes of the slice: x: 4, y: 4, z: 16, core: 2. Of those that a mesh axis runs over, the one named last changes fastest.
Arguments:
- queries: bfloat16 [65536, 4096], P('dp', 'mp'), may hold values from -150 to 150, as said below
- keys: bfloat16 [65536, 4096], P('dp', 'mp'), may hold values from -8 to 8
- values: bfloat16 [65536, 4096], P('dp', 'mp'), may hold values from -6 to 6
- out_weight: bfloat16 [4096, 2048], P('mp', 'dp'), may hold values from -0.375 to 0.375
- span_start: int32 [128], P('dp'), may hold values from 1 to 3
- span_len: int32 [128], P('dp'), may hold values from 1 to 3
Outputs:
- projected: bfloat16 [65536, 2048], P('dp', 'mp')
The draws below stay inside these ranges and needn't reach their ends.
Inputs may be any that keep to these rules, and one draw needn't show every extreme that they name: `queries`: without the hidden law's aligned rows, entries are standard normal values clipped to 8 in magnitude.
All inputs are finite; a program needn't handle non-finite values.
Results may differ from the reference program's by a relative error of at most 0.0068.
Values may be sent and summed in bfloat16 or wider, within the bound.
A program may use at most 64 MiB of HBM per device.

```python
import jax
import jax.numpy as jnp
from jax import lax

HEADS = 32
HD = 128
D = 4096
OUT_WIN = 2048
SEQ = 512
BLK = 128
NB = 4
TOKENS = 65536
N_DP = 128


def paired_rows(key):
    key_rows = jnp.clip(jax.random.normal(jax.random.fold_in(key, 12), (TOKENS, D), jnp.float32), -8.0, 8.0)
    query_rows = jnp.clip(jax.random.normal(jax.random.fold_in(key, 11), (TOKENS, D), jnp.float32), -8.0, 8.0)
    return (query_rows, key_rows)


def draw_queries(key, part):
    return paired_rows(key)[0].astype(jnp.bfloat16)


def draw_keys(key, part):
    return paired_rows(key)[1].astype(jnp.bfloat16)


def plant(values, own_key, low, largest):
    extent = values.shape
    index_at = [jax.random.randint(jax.random.fold_in(own_key, axis), (), 0, extent[axis]) for axis in range(len(extent))]
    values = values.at[tuple(index_at)].set(low)
    longest = extent.index(max(extent))
    index_at[longest] = (index_at[longest] + 1) % extent[longest]
    return values.at[tuple(index_at)].set(largest)


def with_spikes(array, stream_key, source, target, parts, factor):
    def block_of(axis_at):
        return (jnp.arange(array.shape[axis_at]) // (array.shape[axis_at] // parts)).reshape((-1,) + (1,) * (array.ndim - 1 - axis_at))

    near = jax.random.permutation(stream_key, parts)[block_of(target)]
    other_side = (block_of(target) + parts // 2) % parts
    return jnp.where((block_of(source) == near) | (block_of(source) == other_side), factor * array, array)


def level_of(key, extent, pieces, smallest, largest):
    def one(dim, parts):
        draws = jax.random.uniform(jax.random.fold_in(jax.random.fold_in(key, 6), dim), (parts,), jnp.float32, smallest / len(pieces), largest / len(pieces))
        return jnp.repeat(jnp.exp(draws), extent[dim] // parts).reshape((-1,) + (1,) * (len(extent) - dim - 1))

    loudness = one(*pieces[0])
    for cut in pieces[1:]:
        loudness = loudness * one(*cut)
    return loudness


def scatter_about(own_key, shape, spread, limit, shards=(), kind=jnp.bfloat16):
    drawn = spread * jax.random.normal(own_key, shape, jnp.float32)
    if shards:
        drawn = drawn * level_of(own_key, shape, shards, -0.22, 0.18)
    return jnp.clip(drawn, -limit, limit).astype(kind)


def gaussian_with(stream_key, dims, width, most, shards, heavy, kind=jnp.bfloat16):
    values = width * jax.random.normal(stream_key, dims, jnp.float32)
    if shards:
        values = values * level_of(stream_key, dims, shards, -0.22, 0.18)
    return jnp.clip(with_spikes(values, jax.random.fold_in(stream_key, 3), *heavy), -most, most).astype(kind)


def setup_inputs(seed: int = 0) -> dict:
    seeds = jax.random.split(jax.random.key(seed), 7)
    return {
        "queries": draw_queries(jax.random.fold_in(seeds[6], 71), 0),
        "keys": draw_keys(jax.random.fold_in(seeds[6], 71), 0),
        "values": scatter_about(seeds[2], (TOKENS, D), 1.0, 6.0, ((0, 128), (1, 4))),
        "out_weight": gaussian_with(seeds[3], (D, OUT_WIN), D ** -0.5, 0.375, ((0, 4), (1, 128)), (0, 1, 128, 5.5)),
        "span_start": plant(jax.random.randint(seeds[4], (N_DP,), 1, NB), jax.random.fold_in(seeds[4], 1), 1, NB - 1).astype(jnp.int32),
        "span_len": plant(jax.random.randint(seeds[5], (N_DP,), 1, NB), jax.random.fold_in(seeds[5], 1), 1, NB - 1).astype(jnp.int32),
    }


def attend_one(query_rows, key_rows, value_rows, start, length):
    position = jnp.arange(SEQ, dtype=jnp.int32)
    block = position // BLK
    finish = jnp.minimum(start + length, NB)
    image = (block >= start) & (block < finish)
    causal = position[None, :] <= position[:, None]
    allowed = jnp.where(image[:, None], image[None, :], causal)
    query_f = query_rows.reshape(SEQ, HEADS, HD).astype(jnp.float32)
    key_f = key_rows.reshape(SEQ, HEADS, HD).astype(jnp.float32)
    value_f = value_rows.reshape(SEQ, HEADS, HD).astype(jnp.float32)
    scores = jnp.einsum('qhd,khd->hqk', query_f, key_f) / jnp.sqrt(jnp.float32(HD))
    scores = jnp.where(allowed[None, :, :], scores, jnp.float32(-1e+30))
    top = lax.optimization_barrier(jnp.max(scores, axis=-1, keepdims=True))
    expo = jnp.exp(scores - top)
    weights = (expo / lax.optimization_barrier(jnp.sum(expo, axis=-1, keepdims=True))).astype(jnp.bfloat16)
    result = jnp.einsum('hqk,khd->qhd', weights.astype(jnp.float32), value_f)
    return result.astype(jnp.bfloat16).reshape(SEQ, D)

def reference(queries, keys, values, out_weight, span_start, span_len):

    def one(items):
        return attend_one(items[0], items[1], items[2], items[3], items[4])
    attended = lax.map(one, (queries.reshape(N_DP, SEQ, D), keys.reshape(N_DP, SEQ, D), values.reshape(N_DP, SEQ, D), span_start.astype(jnp.int32), span_len.astype(jnp.int32)))
    attended = attended.reshape(TOKENS, D)
    return jnp.dot(attended, out_weight, preferred_element_type=jnp.float32).astype(jnp.bfloat16)
```

```python
import functools

import jax
import jax.numpy as jnp
from jax import lax
from jax.experimental import pallas as pl
from jax.experimental.pallas import tpu as pltpu
from jax.sharding import PartitionSpec as P

MESH = pl.DeviceIdType.MESH
HD = 128
BLK = 128
SEQ = 512
HEADS = 8
FEAT = HEADS * HD
NEG = -1e30
SCALE = 1.4426950408889634 / (128.0**0.5)
TRANS = (((1,), (1,)), ((), ()))


def attend_head(q_ref, k_ref, v_ref, att, bias, h):
    cols = pl.ds(pl.multiple_of(h * HD, HD), HD)
    key = k_ref[:, cols]
    val = v_ref[:, cols]
    for qb in range(SEQ // BLK):
        rows = pl.ds(qb * BLK, BLK)
        keys = BLK if qb == 0 else SEQ
        s = lax.dot_general(q_ref[rows, cols], key[:keys], TRANS, preferred_element_type=jnp.float32)
        s = s + bias[rows, pl.ds(0, keys)]
        top = jnp.max(s, axis=-1, keepdims=True)
        p = jnp.exp2((s - top) * SCALE)
        total = jnp.sum(p, axis=-1, keepdims=True)
        o = jnp.dot(p.astype(jnp.bfloat16), val[:keys], preferred_element_type=jnp.float32)
        att[rows, cols] = (o / total).astype(jnp.bfloat16)


def kernel(start_ref, len_ref, q_hbm, k_hbm, v_hbm, w_hbm, o_ref,
           q, k, v, att, bias, wb, own, xs, xr,
           qsem, wsem, wr, wu, ws, fs, fr, xss, xrs):
    dp, x = lax.axis_index("dp"), lax.axis_index("mp")
    c = lax.rem(dp, 2)
    y = lax.rem(lax.div(dp, 2), 4)
    z = lax.div(dp, 8)
    a0, b0 = lax.div(z, 4), lax.rem(z, 4)
    two = 2 - 4 * lax.rem(z, 2)

    def at(dz=0, dy=0, dx=0, dc=0):
        zz, yy = lax.rem(z + dz + 16, 16), lax.rem(y + dy + 4, 4)
        return ((zz * 4 + yy) * 2 + lax.rem(c + dc, 2), lax.rem(x + dx + 4, 4))

    def group(dz):
        zz = lax.rem(z + dz + 16, 16)
        return lax.div(zz, 4), lax.rem(zz, 4)

    def turn(a, r):
        return lax.rem(a + r + 4, 4)

    barrier = pltpu.get_barrier_semaphore()
    partners = [at(dz=4), at(dz=-4), at(dz=8), at(dz=1), at(dz=-1), at(dz=2), at(dz=-2),
                at(dy=1), at(dy=-1), at(dy=2), at(dx=1), at(dx=2), at(dx=3), at(dc=1)]
    for who in partners:
        pl.semaphore_signal(barrier, inc=1, device_id=who, device_id_type=MESH)

    mine = wb.at[a0, b0, y, c]
    w_in = pltpu.make_async_copy(w_hbm, mine, wsem)
    w_in.start()

    def inputs(i):
        cols = pl.ds(pl.multiple_of(i * 256, 256), 256)
        return [pltpu.make_async_copy(src.at[:, cols], dst.at[:, cols], qsem.at[n, i])
                for n, (src, dst) in enumerate(((q_hbm, q), (k_hbm, k), (v_hbm, v)))]

    for i in range(4):
        for copy in inputs(i):
            copy.start()

    row = lax.broadcasted_iota(jnp.int32, (SEQ, SEQ), 0)
    col = lax.broadcasted_iota(jnp.int32, (SEQ, SEQ), 1)
    first = start_ref[0] * BLK
    last = jnp.minimum(start_ref[0] + len_ref[0], SEQ // BLK) * BLK
    image_row = (row >= first) & (row < last)
    image_col = (col >= first) & (col < last)
    bias[...] = jnp.where(image_row, jnp.where(image_col, 0.0, NEG), jnp.where(col <= row, 0.0, NEG))

    def heads(i, carry):
        for copy in inputs(i):
            copy.wait()
        for j in range(2):
            attend_head(q, k, v, att, bias, i * 2 + j)
        return carry

    lax.fori_loop(0, 2, heads, 0)

    sent = []

    def send(src, dst, sem, who):
        n = len(sent)
        copy = pltpu.make_async_remote_copy(src_ref=src, dst_ref=dst, send_sem=ws.at[n], recv_sem=sem,
                                            device_id=who, device_id_type=MESH)
        copy.start()
        sent.append(copy)

    def piece(a, b, yy, who):
        send(wb.at[a, b, yy, c], wb.at[a, b, yy, c], wr.at[a, b, yy], who)

    def got(ref, sem):
        pltpu.make_async_remote_copy(src_ref=ref, dst_ref=ref, send_sem=ws.at[0], recv_sem=sem,
                                     device_id=at(dc=1), device_id_type=MESH).wait_recv()

    def got_piece(a, b, yy):
        got(wb.at[a, b, yy, c], wr.at[a, b, yy])

    over_y = (1, -1, 2)

    w_in.wait()
    pl.semaphore_wait(barrier, len(partners))
    for dz in (8, 4, -4):
        piece(a0, b0, y, at(dz=dz))
    for dy in over_y:
        piece(a0, b0, y, at(dy=dy))

    lax.fori_loop(2, 4, heads, 0)

    for dy in over_y:
        got_piece(a0, b0, turn(y, dy))
    for dz in (1, -1, two):
        unit = wb.at[a0, b0, :, c]
        send(unit, unit, wu.at[b0], at(dz=dz))
    for r in (1, -1, 2):
        a = turn(a0, r)
        got_piece(a, b0, y)
        for dy in over_y:
            piece(a, b0, y, at(dy=dy))
        for dz in (1, -1, two):
            piece(a, b0, y, at(dz=dz))

    near = (1, -1, -two)

    def relay(dz):
        a, b = group(dz)
        for r in (1, -1, 2):
            ar = turn(a, r)
            got_piece(ar, b, y)
            for dy in over_y:
                piece(ar, b, y, at(dy=dy))

    def whole(dz):
        a, b = group(dz)
        if isinstance(dz, int) and dz == 0:
            pass
        else:
            got(wb.at[a, b, :, c], wu.at[b])
        for r in (1, -1, 2):
            for dy in over_y:
                got_piece(turn(a, r), b, turn(y, dy))
        return b

    def across(b, s):
        copy = pltpu.make_async_remote_copy(src_ref=wb.at[:, b, :, c], dst_ref=wb.at[:, b, :, c], send_sem=fs.at[s],
                                            recv_sem=fr.at[s], device_id=at(dc=1), device_id_type=MESH)
        copy.start()
        sent.append(copy)

    def across_in(b, s):
        other = wb.at[:, b, :, 1 - c]
        got(other, fr.at[s])

    def project(b, s):
        for r in (2, 1, 3, 0):
            a = turn(x, r)
            w = wb[a, b].reshape(128, FEAT)
            part = lax.dot_general(att[...], w, TRANS, preferred_element_type=jnp.float32)
            if r == 0:
                own[s] = part
            else:
                xs[s, r - 1] = part.astype(jnp.bfloat16)
                copy = pltpu.make_async_remote_copy(src_ref=xs.at[s, r - 1], dst_ref=xr.at[s, r - 1],
                                                    send_sem=xss.at[s, r - 1], recv_sem=xrs.at[s, r - 1],
                                                    device_id=at(dx=r), device_id_type=MESH)
                copy.start()
                sent.append(copy)

    def finish(b, s):
        total = own[s]
        for r in range(3):
            got(xr.at[s, r], xrs.at[s, r])
            total = total + xr[s, r].astype(jnp.float32)
        o_ref[:, pl.ds(pl.multiple_of(b * 128, 128), 128)] = total.astype(jnp.bfloat16)

    relay(near[0])
    relay(near[1])
    b_0 = whole(0)
    across(b_0, 0)
    relay(near[2])
    across_in(b_0, 0)
    project(b_0, 0)
    bs = [b_0]
    for s in range(1, 4):
        b = whole(near[s - 1])
        across(b, s)
        across_in(b, s)
        project(b, s)
        bs.append(b)
    for s in range(4):
        finish(bs[s], s)
    for copy in sent:
        copy.wait_send()


def shards(queries, keys, values, out_weight, span_start, span_len):
    any_spec = pl.BlockSpec(memory_space=pl.ANY)
    smem = pl.BlockSpec(memory_space=pltpu.SMEM)
    bf16, f32 = jnp.bfloat16, jnp.float32
    dma = pltpu.SemaphoreType.DMA
    return pl.pallas_call(
        kernel,
        out_shape=jax.ShapeDtypeStruct((SEQ, 512), bf16),
        in_specs=[smem, smem, any_spec, any_spec, any_spec, any_spec],
        out_specs=pl.BlockSpec(memory_space=pltpu.VMEM),
        scratch_shapes=[
            pltpu.VMEM((SEQ, FEAT), bf16),
            pltpu.VMEM((SEQ, FEAT), bf16),
            pltpu.VMEM((SEQ, FEAT), bf16),
            pltpu.VMEM((SEQ, FEAT), bf16),
            pltpu.VMEM((SEQ, SEQ), f32),
            pltpu.VMEM((4, 4, 4, 2, 16, FEAT), bf16),
            pltpu.VMEM((4, SEQ, 128), f32),
            pltpu.VMEM((4, 3, SEQ, 128), bf16),
            pltpu.VMEM((4, 3, SEQ, 128), bf16),
            dma((3, 4)), dma, dma((4, 4, 4)), dma((4,)), dma((64,)), dma((4,)), dma((4,)), dma((4, 3)), dma((4, 3)),
        ],
        compiler_params=pltpu.CompilerParams(
            collective_id=0, has_side_effects=True, vmem_limit_bytes=63 << 20
        ),
        name="attend_project",
    )(span_start, span_len, queries, keys, values, out_weight.T)


def solution(mesh):
    placed = (P("dp", "mp"), P("dp", "mp"), P("dp", "mp"), P("mp", "dp"), P("dp"), P("dp"))
    return jax.shard_map(shards, mesh=mesh, in_specs=placed, out_specs=P("dp", "mp"), check_vma=False)
```

```python
import functools

import jax
import jax.numpy as jnp
from jax import lax
from jax.experimental import pallas as pl
from jax.experimental.pallas import tpu as pltpu
from jax.sharding import PartitionSpec as P

MESH = pl.DeviceIdType.MESH
HD = 128
BLK = 128
SEQ = 512
HEADS = 8
FEAT = HEADS * HD
NEG = -1e30
SCALE = 1.4426950408889634 / (128.0**0.5)
TRANS = (((1,), (1,)), ((), ()))
BEFORE, CUT = 2, 7


def attend_head(q_ref, k_ref, v_ref, att, bias, h):
    cols = pl.ds(pl.multiple_of(h * HD, HD), HD)
    key = k_ref[:, cols]
    val = v_ref[:, cols]
    for qb in range(SEQ // BLK):
        rows = pl.ds(qb * BLK, BLK)
        keys = BLK if qb == 0 else SEQ
        s = lax.dot_general(q_ref[rows, cols], key[:keys], TRANS, preferred_element_type=jnp.float32)
        s = s + bias[rows, pl.ds(0, keys)]
        top = jnp.max(s, axis=-1, keepdims=True)
        p = jnp.exp2((s - top) * SCALE)
        total = jnp.sum(p, axis=-1, keepdims=True)
        o = jnp.dot(p.astype(jnp.bfloat16), val[:keys], preferred_element_type=jnp.float32)
        att[rows, cols] = (o / total).astype(jnp.bfloat16)


def kernel(start_ref, len_ref, q_hbm, k_hbm, v_hbm, w_hbm, o_ref,
           q, k, v, att, bias, wb, own, keep, xs, xm, xf, xr,
           qsem, wsem, wr, wl, wh, wu, wuh, ws, fs, fr, xss, xrs, xms):
    dp, x = lax.axis_index("dp"), lax.axis_index("mp")
    c = lax.rem(dp, 2)
    y = lax.rem(lax.div(dp, 2), 4)
    z = lax.div(dp, 8)
    two = 2 - 4 * lax.rem(z, 2)

    def at(dz=0, dy=0, dx=0, dc=0):
        zz, yy = lax.rem(z + dz + 16, 16), lax.rem(y + dy + 4, 4)
        return ((zz * 4 + yy) * 2 + lax.rem(c + dc, 2), lax.rem(x + dx + 4, 4))

    def turn(a, r):
        return lax.rem(a + r + 4, 4)

    shift = (0, 1, -1, -two)
    zs = [lax.rem(z + d + 16, 16) for d in shift]
    a_of = [lax.div(zz, 4) for zz in zs]
    b_of = [lax.rem(zz, 4) for zz in zs]
    over_y = (1, -1, 2)
    near_z = (1, -1, two)
    lo, hi = pl.ds(0, FEAT // 2), pl.ds(FEAT // 2, FEAT // 2)

    barrier = pltpu.get_barrier_semaphore()
    partners = [at(dz=4), at(dz=-4), at(dz=1), at(dz=-1), at(dz=2), at(dz=-2),
                at(dy=1), at(dy=-1), at(dy=2), at(dx=1), at(dx=2), at(dx=3), at(dc=1)]
    for who in partners:
        pl.semaphore_signal(barrier, inc=1, device_id=who, device_id_type=MESH)

    w_in = pltpu.make_async_copy(w_hbm, wb.at[a_of[0], b_of[0], y, c], wsem)
    w_in.start()

    def inputs(i):
        cols = pl.ds(pl.multiple_of(i * 256, 256), 256)
        return [pltpu.make_async_copy(src.at[:, cols], dst.at[:, cols], qsem.at[n, i])
                for n, (src, dst) in enumerate(((q_hbm, q), (k_hbm, k), (v_hbm, v)))]

    for i in range(4):
        for copy in inputs(i):
            copy.start()

    row = lax.broadcasted_iota(jnp.int32, (SEQ, SEQ), 0)
    col = lax.broadcasted_iota(jnp.int32, (SEQ, SEQ), 1)
    first = start_ref[0] * BLK
    last = jnp.minimum(start_ref[0] + len_ref[0], SEQ // BLK) * BLK
    image_row = (row >= first) & (row < last)
    image_col = (col >= first) & (col < last)
    bias[...] = jnp.where(image_row, jnp.where(image_col, 0.0, NEG), jnp.where(col <= row, 0.0, NEG))

    def heads(from_head, to_head):
        def body(h, carry):
            @pl.when(lax.rem(h, 2) == 0)
            def _():
                for copy in inputs(lax.div(h, 2)):
                    copy.wait()

            attend_head(q, k, v, att, bias, h)
            return carry

        lax.fori_loop(from_head, to_head, body, 0)

    sent = []

    def send(ref, sem, who):
        copy = pltpu.make_async_remote_copy(src_ref=ref, dst_ref=ref, send_sem=ws.at[len(sent)], recv_sem=sem,
                                            device_id=who, device_id_type=MESH)
        copy.start()
        sent.append(copy)

    def got(ref, sem):
        pltpu.make_async_remote_copy(src_ref=ref, dst_ref=ref, send_sem=ws.at[0], recv_sem=sem,
                                     device_id=at(dc=1), device_id_type=MESH).wait_recv()

    def slot(n, r, dy):
        return turn(a_of[n], r), b_of[n], turn(y, dy)

    def whole(n, r, dy):
        i = slot(n, r, dy)
        return wb.at[i[0], i[1], i[2], c], wr.at[i[0], i[1], i[2]]

    def low(n, r, dy):
        i = slot(n, r, dy)
        return wb.at[i[0], i[1], i[2], c, :, lo], wl.at[i[0], i[1], i[2]]

    def high(n, r, dy):
        i = slot(n, r, dy)
        return wb.at[i[0], i[1], i[2], c, :, hi], wh.at[i[0], i[1], i[2]]

    def unit(n, r):
        i = slot(n, r, 0)
        return wb.at[i[0], i[1], :, c], wu.at[i[1]]

    def unit_high(n, r):
        i = slot(n, r, 0)
        return wb.at[i[0], i[1], :, c, :, hi], wuh.at[i[1]]

    def to_y(what):
        for dy in over_y:
            send(*what, at(dy=dy))

    def to_z(what):
        for dz in near_z:
            send(*what, at(dz=dz))

    blocks = []

    def across(n, r):
        i = slot(n, r, 0)
        ref = wb.at[i[0], i[1], :, c]
        m = len(blocks)
        copy = pltpu.make_async_remote_copy(src_ref=ref, dst_ref=ref, send_sem=fs.at[m], recv_sem=fr.at[m],
                                            device_id=at(dc=1), device_id_type=MESH)
        copy.start()
        blocks.append((n, r, copy))

    half = SEQ // 2
    top, low_half = pl.ds(0, half), pl.ds(half, half)

    def hop(m, dst, rows, k, sem, to):
        return pltpu.make_async_remote_copy(src_ref=xs.at[m, rows], dst_ref=dst, send_sem=xss.at[m, k], recv_sem=sem,
                                            device_id=(dp, to), device_id_type=MESH)

    def to_dest(n, m, side, k):
        a = turn(a_of[n], blocks[m][1])
        rows = top if k == 0 else low_half
        return hop(m, xr.at[n, side, k], rows, k, xrs.at[n, side, k], a)

    def to_dest_f(n, m, side, k):
        a = turn(a_of[n], blocks[m][1])
        return pltpu.make_async_remote_copy(src_ref=xf.at[m], dst_ref=xr.at[n, side, k], send_sem=xss.at[m, k],
                                            recv_sem=xrs.at[n, side, k], device_id=(dp, a), device_id_type=MESH)

    def to_middle(m, k):
        rows = top if k == 0 else low_half
        return hop(m, xm.at[m], rows, k, xms.at[m], turn(x, -1 if k == 0 else 1))

    def project(*ms):
        ws_in = []
        for m in ms:
            n, r, _ = blocks[m]
            a, b, _ = slot(n, r, 0)
            got(wb.at[a, b, :, 1 - c], fr.at[m])
            ws_in.append(wb[a, b].reshape(128, FEAT))
        w = ws_in[0] if len(ws_in) == 1 else jnp.concatenate(ws_in, axis=0)
        parts = lax.dot_general(att[...], w, TRANS, preferred_element_type=jnp.float32)
        for k, m in enumerate(ms):
            n, r, _ = blocks[m]
            a = turn(a_of[n], r)
            part = parts[:, k * 128:(k + 1) * 128]

            away = turn(a, -x)

            @pl.when(away == 0)
            def _(n=n, part=part):
                own[n] = part

            @pl.when(away != 0)
            def _(m=m, part=part):
                xs[m] = part.astype(jnp.bfloat16)

            @pl.when(away == 1)
            def _(n=n, m=m, part=part):
                keep[m] = part[half:]
                to_dest(n, m, 1, 0).start()

            @pl.when(away == 3)
            def _(n=n, m=m, part=part):
                keep[m] = part[:half]
                to_dest(n, m, 0, 1).start()

            @pl.when(away == 2)
            def _(m=m):
                to_middle(m, 0).start()
                to_middle(m, 1).start()

    def forward(*ms):
        for m in ms:
            n, r, _ = blocks[m]
            away = turn(turn(a_of[n], r), -x)
            for here, side, k in ((1, 1, 1), (3, 0, 0)):
                @pl.when(away == here)
                def _(n=n, m=m, side=side, k=k):
                    got(xm.at[m], xms.at[m])
                    rows = top if k == 0 else low_half
                    fs_m = (keep[m] + xm[m].astype(jnp.float32)).astype(jnp.bfloat16)
                    xf[m] = fs_m
                    to_dest_f(n, m, side, k).start()

    heads(0, BEFORE)
    w_in.wait()
    pl.semaphore_wait(barrier, len(partners))
    for dz in (4, -4):
        send(*whole(0, 0, 0), at(dz=dz))
    to_y(whole(0, 0, 0))
    to_z(whole(0, 0, 0))
    heads(BEFORE, CUT)
    got(*whole(0, 1, 0))
    got(*whole(0, -1, 0))
    i = slot(0, -1, 0)
    send(wb.at[i[0], i[1], i[2], c, :, lo], wl.at[i[0], i[1], i[2]], at(dz=4))
    i = slot(0, 1, 0)
    send(wb.at[i[0], i[1], i[2], c, :, hi], wh.at[i[0], i[1], i[2]], at(dz=-4))
    to_y(whole(0, 1, 0))
    to_z(whole(0, -1, 0))
    to_y(whole(0, -1, 0))
    for n in (1, 2, 3):
        got(*whole(n, 0, 0))
        to_y(whole(n, 0, 0))
    for dy in over_y:
        got(*whole(0, 0, dy))
    across(0, 0)
    heads(CUT, HEADS)
    project(0)
    for dy in over_y:
        got(*whole(0, 1, dy))
    to_z(unit(0, 1))
    across(0, 1)
    got(*low(0, 2, 0))
    to_z(low(0, 2, 0))
    to_y(low(0, 2, 0))
    got(*high(0, 2, 0))
    to_y(high(0, 2, 0))
    for dy in over_y:
        got(*whole(0, -1, dy))
    across(0, -1)
    for n in (1, 2, 3):
        got(*whole(n, -1, 0))
        to_y(whole(n, -1, 0))
    project(1, 2)
    for n in (1, 2, 3):
        for dy in over_y:
            got(*whole(n, 0, dy))
        across(n, 0)
    forward(0)
    for dy in over_y:
        got(*high(0, 2, dy))
    to_z(unit_high(0, 2))
    for n in (1, 2, 3):
        got(*low(n, 2, 0))
        to_y(low(n, 2, 0))
    for dy in over_y:
        got(*low(0, 2, dy))
    across(0, 2)
    project(3, 4, 5, 6)
    forward(1, 2)
    for n in (1, 2, 3):
        got(*unit(n, 1))
        across(n, 1)
    for n in (1, 2, 3):
        for dy in over_y:
            got(*whole(n, -1, dy))
        across(n, -1)
    project(7, 8, 9, 10)
    forward(3, 4)
    project(11, 12)
    forward(5, 6)
    for n in (1, 2, 3):
        got(*unit_high(n, 2))
        for dy in over_y:
            got(*low(n, 2, dy))
        across(n, 2)
    forward(7, 8)
    project(13, 14, 15)
    forward(9, 10, 11, 12, 13, 14, 15)
    for n in range(4):
        cols = pl.ds(pl.multiple_of(b_of[n] * 128, 128), 128)
        for k, rows in ((0, top), (1, low_half)):
            total = own[n, rows]
            for side in range(2):
                got(xr.at[n, side, k], xrs.at[n, side, k])
                total = total + xr[n, side, k].astype(jnp.float32)
            o_ref[rows, cols] = total.astype(jnp.bfloat16)
    for copy in sent:
        copy.wait_send()
    for m, (n, r, copy) in enumerate(blocks):
        copy.wait_send()
        away = turn(turn(a_of[n], r), -x)

        @pl.when(away == 1)
        def _(n=n, m=m):
            to_dest(n, m, 1, 0).wait_send()
            to_dest_f(n, m, 1, 1).wait_send()

        @pl.when(away == 3)
        def _(n=n, m=m):
            to_dest(n, m, 0, 1).wait_send()
            to_dest_f(n, m, 0, 0).wait_send()

        @pl.when(away == 2)
        def _(m=m):
            to_middle(m, 0).wait_send()
            to_middle(m, 1).wait_send()


def shards(queries, keys, values, out_weight, span_start, span_len):
    any_spec = pl.BlockSpec(memory_space=pl.ANY)
    smem = pl.BlockSpec(memory_space=pltpu.SMEM)
    bf16, f32 = jnp.bfloat16, jnp.float32
    dma = pltpu.SemaphoreType.DMA
    return pl.pallas_call(
        kernel,
        out_shape=jax.ShapeDtypeStruct((SEQ, 512), bf16),
        in_specs=[smem, smem, any_spec, any_spec, any_spec, any_spec],
        out_specs=pl.BlockSpec(memory_space=pltpu.VMEM),
        scratch_shapes=[
            pltpu.VMEM((SEQ, FEAT), bf16),
            pltpu.VMEM((SEQ, FEAT), bf16),
            pltpu.VMEM((SEQ, FEAT), bf16),
            pltpu.VMEM((SEQ, FEAT), bf16),
            pltpu.VMEM((SEQ, SEQ), f32),
            pltpu.VMEM((4, 4, 4, 2, 16, FEAT), bf16),
            pltpu.VMEM((4, SEQ, 128), f32),
            pltpu.VMEM((16, SEQ // 2, 128), f32),
            pltpu.VMEM((16, SEQ, 128), bf16),
            pltpu.VMEM((16, SEQ // 2, 128), bf16),
            pltpu.VMEM((16, SEQ // 2, 128), bf16),
            pltpu.VMEM((4, 2, 2, SEQ // 2, 128), bf16),
            dma((3, 4)), dma, dma((4, 4, 4)), dma((4, 4, 4)), dma((4, 4, 4)), dma((4,)), dma((4,)), dma((64,)),
            dma((16,)), dma((16,)), dma((16, 2)), dma((4, 2, 2)), dma((16,)),
        ],
        compiler_params=pltpu.CompilerParams(
            collective_id=0, has_side_effects=True, vmem_limit_bytes=63 << 20
        ),
        name="attend_project",
    )(span_start, span_len, queries, keys, values, out_weight.T)


def solution(mesh):
    placed = (P("dp", "mp"), P("dp", "mp"), P("dp", "mp"), P("mp", "dp"), P("dp"), P("dp"))
    return jax.shard_map(shards, mesh=mesh, in_specs=placed, out_specs=P("dp", "mp"), check_vma=False)
```

```python
import functools

import jax
import jax.numpy as jnp
from jax import lax
from jax.experimental import pallas as pl
from jax.experimental.pallas import tpu as pltpu
from jax.sharding import PartitionSpec as P

MESH = pl.DeviceIdType.MESH
HD = 128
BLK = 128
SEQ = 512
HEADS = 8
FEAT = HEADS * HD
NEG = -1e30
SCALE = 1.4426950408889634 / (128.0**0.5)
TRANS = (((1,), (1,)), ((), ()))
BEFORE, CUT1, CUT2 = 2, 5, 7
VMEM_BYTES = 63 << 20


def attend_head(q_ref, k_ref, v_ref, att, bias, h):
    cols = pl.ds(pl.multiple_of(h * HD, HD), HD)
    key = k_ref[:, cols]
    val = v_ref[:, cols]
    for qb in range(SEQ // BLK):
        rows = pl.ds(qb * BLK, BLK)
        keys = BLK if qb == 0 else SEQ
        s = lax.dot_general(q_ref[rows, cols], key[:keys], TRANS, preferred_element_type=jnp.float32)
        s = s + bias[rows, pl.ds(0, keys)]
        top = jnp.max(s, axis=-1, keepdims=True)
        p = jnp.exp2((s - top) * SCALE)
        total = jnp.sum(p, axis=-1, keepdims=True)
        o = jnp.dot(p.astype(jnp.bfloat16), val[:keys], preferred_element_type=jnp.float32)
        att[rows, cols] = (o / total).astype(jnp.bfloat16)


def kernel(start_ref, len_ref, q_hbm, k_hbm, v_hbm, w_hbm, o_hbm,
           qkv, att, bias, wb, own, keep, xs, xm, xf, xr, out,
           osem, qsem, wsem, here_sem, y_sem, unit_sem, ws, fs, fr, xss, xrs, xms):
    dp, x = lax.axis_index("dp"), lax.axis_index("mp")
    c = lax.rem(dp, 2)
    y = lax.rem(lax.div(dp, 2), 4)
    z = lax.div(dp, 8)
    two = 2 - 4 * lax.rem(z, 2)

    def at(dz=0, dy=0, dx=0, dc=0):
        zz, yy = lax.rem(z + dz + 16, 16), lax.rem(y + dy + 4, 4)
        return ((zz * 4 + yy) * 2 + lax.rem(c + dc, 2), lax.rem(x + dx + 4, 4))

    def turn(a, r):
        return lax.rem(a + r + 4, 4)

    shift = (0, 1, -1, -two)
    zs = [lax.rem(z + d + 16, 16) for d in shift]
    a_of = [lax.div(zz, 4) for zz in zs]
    b_of = [lax.rem(zz, 4) for zz in zs]
    over_y = (1, -1, 2)
    near_z = (1, -1, two)
    lo, hi = pl.ds(0, FEAT // 2), pl.ds(FEAT // 2, FEAT // 2)

    barrier = pltpu.get_barrier_semaphore()
    partners = [at(dz=4), at(dz=-4), at(dz=1), at(dz=-1), at(dz=2), at(dz=-2),
                at(dy=1), at(dy=-1), at(dy=2), at(dx=1), at(dx=2), at(dx=3), at(dc=1)]
    for who in partners:
        pl.semaphore_signal(barrier, inc=1, device_id=who, device_id_type=MESH)

    w_in = pltpu.make_async_copy(w_hbm, wb.at[a_of[0], b_of[0], y, c], wsem)
    w_in.start()

    def quarter(i):
        return pl.ds(pl.multiple_of(i * 256, 256), 256)

    for i in range(4):
        for n, src in enumerate((q_hbm, k_hbm, v_hbm)):
            pltpu.make_async_copy(src.at[:, quarter(i)], qkv.at[n, :, quarter(i)], qsem.at[i]).start()

    row = lax.broadcasted_iota(jnp.int32, (SEQ, SEQ), 0)
    col = lax.broadcasted_iota(jnp.int32, (SEQ, SEQ), 1)
    first = start_ref[0] * BLK
    last = jnp.minimum(start_ref[0] + len_ref[0], SEQ // BLK) * BLK
    image_row = (row >= first) & (row < last)
    image_col = (col >= first) & (col < last)
    bias[...] = jnp.where(image_row, jnp.where(image_col, 0.0, NEG), jnp.where(col <= row, 0.0, NEG))

    def heads(from_head, to_head):
        def body(h, carry):
            @pl.when(lax.rem(h, 2) == 0)
            def _():
                i = lax.div(h, 2)
                pltpu.make_async_copy(qkv.at[:, :, quarter(i)], qkv.at[:, :, quarter(i)], qsem.at[i]).wait()

            attend_head(qkv.at[0], qkv.at[1], qkv.at[2], att, bias, h)
            return carry

        lax.fori_loop(from_head, to_head, body, 0)

    groups = []

    def send(ref, sem, whom, all_of):
        n = len(groups)
        for who in whom:
            pltpu.make_async_remote_copy(src_ref=ref, dst_ref=ref, send_sem=ws.at[n], recv_sem=sem,
                                         device_id=who, device_id_type=MESH).start()
        groups.append(all_of)

    def gone(n):
        pltpu.make_async_remote_copy(src_ref=groups[n], dst_ref=groups[n], send_sem=ws.at[n], recv_sem=ws.at[n],
                                     device_id=at(dc=1), device_id_type=MESH).wait_send()

    def got(ref, sem):
        pltpu.make_async_remote_copy(src_ref=ref, dst_ref=ref, send_sem=ws.at[0], recv_sem=sem,
                                     device_id=at(dc=1), device_id_type=MESH).wait_recv()

    every = pl.ds(0, FEAT)
    three = pl.ds(0, 3)
    kind = {(0, 0): (0, every), (1, 0): (1, every), (-1, 0): (2, every), (2, 0): (3, lo), (2, 1): (4, hi)}

    def piece(n, r, part=0):
        a, b = turn(a_of[n], r), b_of[n]
        sem, feats = kind[r, part]
        return wb.at[a, b, y, c, :, feats], sem, wb.at[a, b, three, c, :, feats]

    def to_y(n, r, part=0):
        ref, sem, size = piece(n, r, part)
        send(ref, y_sem.at[b_of[n], sem], [at(dy=dy) for dy in over_y], size)

    def to_z(n, r, part=0):
        ref, sem, size = piece(n, r, part)
        send(ref, here_sem.at[b_of[n], sem], [at(dz=dz) for dz in near_z], size)

    def got_here(n, r, part=0):
        ref, sem, _ = piece(n, r, part)
        got(ref, here_sem.at[b_of[n], sem])

    def got_y(n, r, part=0):
        _, sem, size = piece(n, r, part)
        got(size, y_sem.at[b_of[n], sem])

    def unit(n, r):
        a, b = turn(a_of[n], r), b_of[n]
        sem, feats = (0, every) if r == 1 else (1, hi)
        return wb.at[a, b, :, c, :, feats], unit_sem.at[b, sem], wb.at[three, b, :, c, :, feats]

    def unit_to_z(r):
        ref, sem, size = unit(0, r)
        send(ref, sem, [at(dz=dz) for dz in near_z], size)

    def got_unit(n, r):
        ref, sem, _ = unit(n, r)
        got(ref, sem)

    blocks = []

    def across(n, r, g):
        ref = wb.at[turn(a_of[n], r), b_of[n], :, c]
        pltpu.make_async_remote_copy(src_ref=ref, dst_ref=ref, send_sem=fs, recv_sem=fr.at[g],
                                     device_id=at(dc=1), device_id_type=MESH).start()
        blocks.append((n, r))

    half = SEQ // 2
    top, low_half = pl.ds(0, half), pl.ds(half, half)

    def hop(m, dst, rows, k, sem, to):
        return pltpu.make_async_remote_copy(src_ref=xs.at[m, rows], dst_ref=dst, send_sem=xss, recv_sem=sem,
                                            device_id=(dp, to), device_id_type=MESH)

    def to_dest(n, m, side, k):
        a = turn(a_of[n], blocks[m][1])
        rows = top if k == 0 else low_half
        return hop(m, xr.at[n, side, k], rows, k, xrs.at[n], a)

    def to_dest_f(n, m, side, k):
        a = turn(a_of[n], blocks[m][1])
        return pltpu.make_async_remote_copy(src_ref=xf.at[m], dst_ref=xr.at[n, side, k], send_sem=xss,
                                            recv_sem=xrs.at[n], device_id=(dp, a), device_id_type=MESH)

    def to_middle(m, k):
        rows = top if k == 0 else low_half
        return hop(m, xm.at[m], rows, k, xms.at[m], turn(x, -1 if k == 0 else 1))

    def project(g, *ms):
        got(wb.at[pl.ds(0, len(ms)), 0, :, 1 - c], fr.at[g])
        ws_in = []
        for m in ms:
            n, r = blocks[m]
            ws_in.append(wb[turn(a_of[n], r), b_of[n]].reshape(128, FEAT))
        w = ws_in[0] if len(ws_in) == 1 else jnp.concatenate(ws_in, axis=0)
        parts = lax.dot_general(att[...], w, TRANS, preferred_element_type=jnp.float32)
        for k, m in enumerate(ms):
            n, r = blocks[m]
            a = turn(a_of[n], r)
            part = parts[:, k * 128:(k + 1) * 128]

            away = turn(a, -x)

            @pl.when(away == 0)
            def _(n=n, part=part):
                own[n] = part

            @pl.when(away != 0)
            def _(m=m, part=part):
                xs[m] = part.astype(jnp.bfloat16)

            @pl.when(away == 1)
            def _(n=n, m=m, part=part):
                keep[m] = part[half:]
                to_dest(n, m, 1, 0).start()

            @pl.when(away == 3)
            def _(n=n, m=m, part=part):
                keep[m] = part[:half]
                to_dest(n, m, 0, 1).start()

            @pl.when(away == 2)
            def _(m=m):
                to_middle(m, 0).start()
                to_middle(m, 1).start()

    def forward(*ms):
        for m in ms:
            n, r = blocks[m]
            away = turn(turn(a_of[n], r), -x)
            for here, side, k in ((1, 1, 1), (3, 0, 0)):
                @pl.when(away == here)
                def _(n=n, m=m, side=side, k=k):
                    got(xm.at[m], xms.at[m])
                    rows = top if k == 0 else low_half
                    fs_m = (keep[m] + xm[m].astype(jnp.float32)).astype(jnp.bfloat16)
                    xf[m] = fs_m
                    to_dest_f(n, m, side, k).start()

    heads(0, BEFORE)
    w_in.wait()
    pl.semaphore_wait(barrier, len(partners))
    to_z(0, 0)
    mine = wb.at[a_of[0], b_of[0], y, c]
    n_out = len(groups)
    for dz, sem in ((4, 2), (-4, 1)):
        pltpu.make_async_remote_copy(src_ref=mine, dst_ref=mine, send_sem=ws.at[n_out],
                                     recv_sem=here_sem.at[b_of[0], sem],
                                     device_id=at(dz=dz), device_id_type=MESH).start()
    groups.append(wb.at[a_of[0], b_of[0], pl.ds(0, 2), c])
    to_y(0, 0)
    heads(BEFORE, CUT1)
    for n in (1, 2, 3):
        got_here(n, 0)
        to_y(n, 0)
    heads(CUT1, CUT2)
    got_here(0, 1)
    got_here(0, -1)
    n_out = len(groups)
    for r, dz, feats, sem in ((-1, 4, lo, 3), (1, -4, hi, 4)):
        ref = wb.at[turn(a_of[0], r), b_of[0], y, c, :, feats]
        pltpu.make_async_remote_copy(src_ref=ref, dst_ref=ref, send_sem=ws.at[n_out],
                                     recv_sem=here_sem.at[b_of[0], sem],
                                     device_id=at(dz=dz), device_id_type=MESH).start()
    groups.append(wb.at[a_of[0], b_of[0], y, c])
    to_y(0, 1)
    to_z(0, -1)
    to_y(0, -1)
    got_y(0, 0)
    across(0, 0, 0)
    heads(CUT2, HEADS)
    project(0, 0)
    for n in (1, 2, 3):
        got_y(n, 0)
        across(n, 0, 1)
    got_y(0, 1)
    unit_to_z(1)
    across(0, 1, 1)
    got_here(0, 2)
    to_z(0, 2)
    to_y(0, 2)
    got_here(0, 2, 1)
    to_y(0, 2, 1)
    for n in (1, 2, 3):
        got_here(n, -1)
        to_y(n, -1)
    project(1, 1, 2, 3, 4)
    got_y(0, -1)
    across(0, -1, 2)
    forward(0)
    for n in (1, 2, 3):
        got_here(n, 2)
        to_y(n, 2)
    got_y(0, 2, 1)
    unit_to_z(2)
    project(2, 5)
    got_y(0, 2)
    across(0, 2, 3)
    for n in (1, 2, 3):
        got_unit(n, 1)
        across(n, 1, 3)
    forward(1, 2)
    for n in (1, 2, 3):
        got_y(n, -1)
        across(n, -1, 4)
    project(3, 6, 7, 8, 9)
    forward(3, 4, 5)
    for n in (1, 2, 3):
        got_unit(n, 2)
        got_y(n, 2)
        across(n, 2, 5)
    project(4, 10, 11, 12)
    project(5, 13, 14, 15)
    for m in range(6, 16):
        forward(m)
        if m > 8:
            for n in range(3 * m - 27, 3 * m - 24):
                gone(n)
    for n in range(21, len(groups)):
        gone(n)
    for n in range(4):
        cols = pl.ds(pl.multiple_of(b_of[n] * 128, 128), 128)
        got(xr.at[n], xrs.at[n])
        for k, rows in ((0, top), (1, low_half)):
            total = own[n, rows]
            for side in range(2):
                total = total + xr[n, side, k].astype(jnp.float32)
            out[rows, cols] = total.astype(jnp.bfloat16)
        pltpu.make_async_copy(out.at[:, cols], o_hbm.at[:, cols], osem).start()
    both = wb.at[:, :, :, c]
    pltpu.make_async_remote_copy(src_ref=both, dst_ref=both, send_sem=fs, recv_sem=fs,
                                 device_id=at(dc=1), device_id_type=MESH).wait_send()
    most = xs.at[pl.ds(0, 12)]
    pltpu.make_async_remote_copy(src_ref=most, dst_ref=most, send_sem=xss, recv_sem=xss,
                                 device_id=at(dc=1), device_id_type=MESH).wait_send()
    pltpu.make_async_copy(out, o_hbm, osem).wait()


def shards(queries, keys, values, out_weight, span_start, span_len):
    hbm = pl.BlockSpec(memory_space=pltpu.HBM)
    smem = pl.BlockSpec(memory_space=pltpu.SMEM)
    bf16, f32 = jnp.bfloat16, jnp.float32
    dma = pltpu.SemaphoreType.DMA
    return pl.pallas_call(
        kernel,
        out_shape=jax.ShapeDtypeStruct((SEQ, 512), bf16),
        in_specs=[smem, smem, hbm, hbm, hbm, hbm],
        out_specs=hbm,
        scratch_shapes=[
            pltpu.VMEM((3, SEQ, FEAT), bf16),
            pltpu.VMEM((SEQ, FEAT), bf16),
            pltpu.VMEM((SEQ, SEQ), f32),
            pltpu.VMEM((4, 4, 4, 2, 16, FEAT), bf16),
            pltpu.VMEM((4, SEQ, 128), f32),
            pltpu.VMEM((16, SEQ // 2, 128), f32),
            pltpu.VMEM((16, SEQ, 128), bf16),
            pltpu.VMEM((16, SEQ // 2, 128), bf16),
            pltpu.VMEM((16, SEQ // 2, 128), bf16),
            pltpu.VMEM((4, 2, 2, SEQ // 2, 128), bf16),
            pltpu.VMEM((SEQ, 512), bf16),
            dma, dma((4,)), dma, dma((4, 5)), dma((4, 5)), dma((4, 2)), dma((24,)), dma, dma((6,)), dma, dma((4,)), dma((16,)),
        ],
        compiler_params=pltpu.CompilerParams(
            collective_id=0, has_side_effects=True, vmem_limit_bytes=VMEM_BYTES
        ),
        name="attend_project",
    )(span_start, span_len, queries, keys, values, out_weight.T)


def solution(mesh):
    placed = (P("dp", "mp"), P("dp", "mp"), P("dp", "mp"), P("mp", "dp"), P("dp"), P("dp"))
    return jax.shard_map(shards, mesh=mesh, in_specs=placed, out_specs=P("dp", "mp"), check_vma=False)
```

```python
import functools

import jax
import jax.numpy as jnp
from jax import lax
from jax.experimental import pallas as pl
from jax.experimental.pallas import tpu as pltpu
from jax.sharding import PartitionSpec as P

MESH = pl.DeviceIdType.MESH
HD = 128
BLK = 128
SEQ = 512
HEADS = 8
FEAT = HEADS * HD
NEG = -1e30
SCALE = 1.4426950408889634 / (128.0**0.5)
TRANS = (((1,), (1,)), ((), ()))
BEFORE, CUT1, CUT2 = 2, 5, 7
VMEM_BYTES = 53 << 20


def attend_head(q_ref, k_ref, v_ref, att, bias, h):
    cols = pl.ds(pl.multiple_of(h * HD, HD), HD)
    key = k_ref[:, cols]
    val = v_ref[:, cols]
    for qb in range(SEQ // BLK):
        rows = pl.ds(qb * BLK, BLK)
        keys = BLK if qb == 0 else SEQ
        s = lax.dot_general(q_ref[rows, cols], key[:keys], TRANS, preferred_element_type=jnp.float32)
        s = s + bias[rows, pl.ds(0, keys)]
        top = jnp.max(s, axis=-1, keepdims=True)
        p = jnp.exp2((s - top) * SCALE)
        total = jnp.sum(p, axis=-1, keepdims=True)
        o = jnp.dot(p.astype(jnp.bfloat16), val[:keys], preferred_element_type=jnp.float32)
        att[rows, cols] = (o / total).astype(jnp.bfloat16)


def kernel(start_ref, len_ref, q_hbm, k_hbm, v_hbm, w_hbm, o_hbm,
           qkv, att, bias, wb, own, keep, xs, xm, xf, xr, out,
           osem, qsem, wsem, here_sem, y_sem, unit_sem, ws, fs, fr, xss, xrs, xms):
    dp, x = lax.axis_index("dp"), lax.axis_index("mp")
    c = lax.rem(dp, 2)
    y = lax.rem(lax.div(dp, 2), 4)
    z = lax.div(dp, 8)
    two = 2 - 4 * lax.rem(z, 2)

    def at(dz=0, dy=0, dx=0, dc=0):
        zz, yy = lax.rem(z + dz + 16, 16), lax.rem(y + dy + 4, 4)
        return ((zz * 4 + yy) * 2 + lax.rem(c + dc, 2), lax.rem(x + dx + 4, 4))

    def turn(a, r):
        return lax.rem(a + r + 4, 4)

    shift = (0, 1, -1, -two)
    zs = [lax.rem(z + d + 16, 16) for d in shift]
    a_of = [lax.div(zz, 4) for zz in zs]
    b_of = [lax.rem(zz, 4) for zz in zs]
    over_y = (1, -1, 2)
    near_z = (1, -1, two)
    lo, hi = pl.ds(0, FEAT // 2), pl.ds(FEAT // 2, FEAT // 2)

    barrier = pltpu.get_barrier_semaphore()
    partners = [at(dz=4), at(dz=-4), at(dz=1), at(dz=-1), at(dz=2), at(dz=-2),
                at(dy=1), at(dy=-1), at(dy=2), at(dx=1), at(dx=2), at(dx=3), at(dc=1)]
    for who in partners:
        pl.semaphore_signal(barrier, inc=1, device_id=who, device_id_type=MESH)

    w_in = pltpu.make_async_copy(w_hbm, wb.at[a_of[0], b_of[0], y, c], wsem)
    w_in.start()

    def quarter(i):
        return pl.ds(pl.multiple_of(i * 256, 256), 256)

    for i in range(4):
        for n, src in enumerate((q_hbm, k_hbm, v_hbm)):
            pltpu.make_async_copy(src.at[:, quarter(i)], qkv.at[n, :, quarter(i)], qsem.at[i]).start()

    row = lax.broadcasted_iota(jnp.int32, (SEQ, SEQ), 0)
    col = lax.broadcasted_iota(jnp.int32, (SEQ, SEQ), 1)
    first = start_ref[0] * BLK
    last = jnp.minimum(start_ref[0] + len_ref[0], SEQ // BLK) * BLK
    image_row = (row >= first) & (row < last)
    image_col = (col >= first) & (col < last)
    bias[...] = jnp.where(image_row, jnp.where(image_col, 0.0, NEG), jnp.where(col <= row, 0.0, NEG))

    def heads(from_head, to_head):
        def body(h, carry):
            @pl.when(lax.rem(h, 2) == 0)
            def _():
                i = lax.div(h, 2)
                pltpu.make_async_copy(qkv.at[:, :, quarter(i)], qkv.at[:, :, quarter(i)], qsem.at[i]).wait()

            attend_head(qkv.at[0], qkv.at[1], qkv.at[2], att, bias, h)
            return carry

        lax.fori_loop(from_head, to_head, body, 0)

    groups = []

    def send(ref, sem, whom, all_of):
        n = len(groups)
        for who in whom:
            pltpu.make_async_remote_copy(src_ref=ref, dst_ref=ref, send_sem=ws.at[n], recv_sem=sem,
                                         device_id=who, device_id_type=MESH).start()
        groups.append(all_of)

    def gone(n):
        pltpu.make_async_remote_copy(src_ref=groups[n], dst_ref=groups[n], send_sem=ws.at[n], recv_sem=ws.at[n],
                                     device_id=at(dc=1), device_id_type=MESH).wait_send()

    def got(ref, sem):
        pltpu.make_async_remote_copy(src_ref=ref, dst_ref=ref, send_sem=ws.at[0], recv_sem=sem,
                                     device_id=at(dc=1), device_id_type=MESH).wait_recv()

    every = pl.ds(0, FEAT)
    three = pl.ds(0, 3)
    kind = {(0, 0): (0, every), (1, 0): (1, every), (-1, 0): (2, every), (2, 0): (3, lo), (2, 1): (4, hi)}

    def piece(n, r, part=0):
        a, b = turn(a_of[n], r), b_of[n]
        sem, feats = kind[r, part]
        return wb.at[a, b, y, c, :, feats], sem, wb.at[a, b, three, c, :, feats]

    def to_y(n, r, part=0):
        ref, sem, size = piece(n, r, part)
        send(ref, y_sem.at[b_of[n], sem], [at(dy=dy) for dy in over_y], size)

    def to_z(n, r, part=0):
        ref, sem, size = piece(n, r, part)
        send(ref, here_sem.at[b_of[n], sem], [at(dz=dz) for dz in near_z], size)

    def got_here(n, r, part=0):
        ref, sem, _ = piece(n, r, part)
        got(ref, here_sem.at[b_of[n], sem])

    def got_y(n, r, part=0):
        _, sem, size = piece(n, r, part)
        got(size, y_sem.at[b_of[n], sem])

    def rest(n, r):
        sem, feats = (0, every) if r == 1 else (1, hi)
        a, b = turn(a_of[n], r), b_of[n]
        return a, b, feats, unit_sem.at[b, sem]

    def rest_to_z(r):
        a, b, feats, sem = rest(0, r)
        m = len(groups)
        for dy in over_y:
            ref = wb.at[a, b, turn(y, dy), c, :, feats]
            for dz in near_z:
                pltpu.make_async_remote_copy(src_ref=ref, dst_ref=ref, send_sem=ws.at[m], recv_sem=sem,
                                             device_id=at(dz=dz), device_id_type=MESH).start()
        groups.append(wb.at[three, b, three, c, :, feats])

    def got_rest(n, r):
        a, b, feats, sem = rest(n, r)
        got(wb.at[a, b, three, c, :, feats], sem)

    blocks = []

    def across(n, r, g):
        ref = wb.at[turn(a_of[n], r), b_of[n], :, c]
        pltpu.make_async_remote_copy(src_ref=ref, dst_ref=ref, send_sem=fs, recv_sem=fr.at[g],
                                     device_id=at(dc=1), device_id_type=MESH).start()
        blocks.append((n, r))

    half = SEQ // 2
    top, low_half = pl.ds(0, half), pl.ds(half, half)

    def hop(m, dst, rows, k, sem, to):
        return pltpu.make_async_remote_copy(src_ref=xs.at[m, rows], dst_ref=dst, send_sem=xss, recv_sem=sem,
                                            device_id=(dp, to), device_id_type=MESH)

    def to_dest(n, m, side, k):
        a = turn(a_of[n], blocks[m][1])
        rows = top if k == 0 else low_half
        return hop(m, xr.at[n, side, k], rows, k, xrs.at[n], a)

    def to_dest_f(n, m, side, k):
        a = turn(a_of[n], blocks[m][1])
        return pltpu.make_async_remote_copy(src_ref=xf.at[m], dst_ref=xr.at[n, side, k], send_sem=xss,
                                            recv_sem=xrs.at[n], device_id=(dp, a), device_id_type=MESH)

    def to_middle(m, k):
        rows = top if k == 0 else low_half
        return hop(m, xm.at[m], rows, k, xms.at[m], turn(x, -1 if k == 0 else 1))

    def project(g, *ms):
        got(wb.at[pl.ds(0, len(ms)), 0, :, 1 - c], fr.at[g])
        ws_in = []
        for m in ms:
            n, r = blocks[m]
            ws_in.append(wb[turn(a_of[n], r), b_of[n]].reshape(128, FEAT))
        w = ws_in[0] if len(ws_in) == 1 else jnp.concatenate(ws_in, axis=0)
        parts = lax.dot_general(att[...], w, TRANS, preferred_element_type=jnp.float32)
        for k, m in enumerate(ms):
            n, r = blocks[m]
            a = turn(a_of[n], r)
            part = parts[:, k * 128:(k + 1) * 128]

            away = turn(a, -x)

            @pl.when(away == 0)
            def _(n=n, part=part):
                own[n] = part

            @pl.when(away != 0)
            def _(m=m, part=part):
                xs[m] = part.astype(jnp.bfloat16)

            @pl.when(away == 1)
            def _(n=n, m=m, part=part):
                keep[m] = part[half:]
                to_dest(n, m, 1, 0).start()

            @pl.when(away == 3)
            def _(n=n, m=m, part=part):
                keep[m] = part[:half]
                to_dest(n, m, 0, 1).start()

            @pl.when(away == 2)
            def _(m=m):
                to_middle(m, 0).start()
                to_middle(m, 1).start()

    def forward(*ms):
        for m in ms:
            n, r = blocks[m]
            away = turn(turn(a_of[n], r), -x)
            for here, side, k in ((1, 1, 1), (3, 0, 0)):
                @pl.when(away == here)
                def _(n=n, m=m, side=side, k=k):
                    got(xm.at[m], xms.at[m])
                    rows = top if k == 0 else low_half
                    fs_m = (keep[m] + xm[m].astype(jnp.float32)).astype(jnp.bfloat16)
                    xf[m] = fs_m
                    to_dest_f(n, m, side, k).start()

    heads(0, BEFORE)
    w_in.wait()
    pl.semaphore_wait(barrier, len(partners))
    to_z(0, 0)
    mine = wb.at[a_of[0], b_of[0], y, c]
    n_out = len(groups)
    for dz, sem in ((4, 2), (-4, 1)):
        pltpu.make_async_remote_copy(src_ref=mine, dst_ref=mine, send_sem=ws.at[n_out],
                                     recv_sem=here_sem.at[b_of[0], sem],
                                     device_id=at(dz=dz), device_id_type=MESH).start()
    groups.append(wb.at[a_of[0], b_of[0], pl.ds(0, 2), c])
    to_y(0, 0)
    heads(BEFORE, CUT1)
    for n in (1, 2, 3):
        got_here(n, 0)
        to_y(n, 0)
    heads(CUT1, CUT2)
    got_here(0, 1)
    got_here(0, -1)
    n_out = len(groups)
    for r, dz, feats, sem in ((-1, 4, lo, 3), (1, -4, hi, 4)):
        ref = wb.at[turn(a_of[0], r), b_of[0], y, c, :, feats]
        pltpu.make_async_remote_copy(src_ref=ref, dst_ref=ref, send_sem=ws.at[n_out],
                                     recv_sem=here_sem.at[b_of[0], sem],
                                     device_id=at(dz=dz), device_id_type=MESH).start()
    groups.append(wb.at[a_of[0], b_of[0], y, c])
    to_y(0, 1)
    to_z(0, 1)
    to_y(0, -1)
    to_z(0, -1)
    got_y(0, 0)
    across(0, 0, 0)
    heads(CUT2, HEADS)
    for n in (1, 2, 3):
        got_y(n, 0)
        across(n, 0, 1)
    project(0, 0)
    got_y(0, 1)
    across(0, 1, 1)
    got_here(0, 2)
    to_z(0, 2)
    to_y(0, 2)
    got_here(0, 2, 1)
    to_z(0, 2, 1)
    to_y(0, 2, 1)
    rest_to_z(1)
    for n in (1, 2, 3):
        got_here(n, -1)
        to_y(n, -1)
    got_y(0, -1)
    across(0, -1, 2)
    project(1, 1, 2, 3, 4)
    forward(0)
    for n in (1, 2, 3):
        got_here(n, 2)
        to_y(n, 2)
    project(2, 5)
    got_y(0, 2, 1)
    rest_to_z(2)
    got_y(0, 2)
    across(0, 2, 3)
    for n in (1, 2, 3):
        got_here(n, 1)
        got_rest(n, 1)
        across(n, 1, 3)
    for n in (1, 2, 3):
        got_y(n, -1)
        across(n, -1, 4)
    forward(1, 2)
    project(3, 6, 7, 8, 9)
    project(4, 10, 11, 12)
    forward(3, 4, 5)
    for n in (1, 2, 3):
        got_here(n, 2, 1)
        got_rest(n, 2)
        got_y(n, 2)
        across(n, 2, 5)
    project(5, 13, 14, 15)
    for m in range(6, 16):
        forward(m)
        if m > 8:
            for n in range(3 * m - 27, 3 * m - 24):
                gone(n)
    for n in range(21, len(groups)):
        gone(n)
    for n in range(4):
        cols = pl.ds(pl.multiple_of(b_of[n] * 128, 128), 128)
        got(xr.at[n], xrs.at[n])
        for k, rows in ((0, top), (1, low_half)):
            total = own[n, rows]
            for side in range(2):
                total = total + xr[n, side, k].astype(jnp.float32)
            out[rows, cols] = total.astype(jnp.bfloat16)
        pltpu.make_async_copy(out.at[:, cols], o_hbm.at[:, cols], osem).start()
    both = wb.at[:, :, :, c]
    pltpu.make_async_remote_copy(src_ref=both, dst_ref=both, send_sem=fs, recv_sem=fs,
                                 device_id=at(dc=1), device_id_type=MESH).wait_send()
    most = xs.at[pl.ds(0, 12)]
    pltpu.make_async_remote_copy(src_ref=most, dst_ref=most, send_sem=xss, recv_sem=xss,
                                 device_id=at(dc=1), device_id_type=MESH).wait_send()
    pltpu.make_async_copy(out, o_hbm, osem).wait()


def shards(queries, keys, values, out_weight, span_start, span_len):
    hbm = pl.BlockSpec(memory_space=pltpu.HBM)
    smem = pl.BlockSpec(memory_space=pltpu.SMEM)
    bf16, f32 = jnp.bfloat16, jnp.float32
    dma = pltpu.SemaphoreType.DMA
    return pl.pallas_call(
        kernel,
        out_shape=jax.ShapeDtypeStruct((SEQ, 512), bf16),
        in_specs=[smem, smem, hbm, hbm, hbm, hbm],
        out_specs=pl.BlockSpec(memory_space=pl.ANY),
        scratch_shapes=[
            pltpu.VMEM((3, SEQ, FEAT), bf16),
            pltpu.VMEM((SEQ, FEAT), bf16),
            pltpu.VMEM((SEQ, SEQ), f32),
            pltpu.VMEM((4, 4, 4, 2, 16, FEAT), bf16),
            pltpu.VMEM((4, SEQ, 128), f32),
            pltpu.VMEM((16, SEQ // 2, 128), f32),
            pltpu.VMEM((16, SEQ, 128), bf16),
            pltpu.VMEM((16, SEQ // 2, 128), bf16),
            pltpu.VMEM((16, SEQ // 2, 128), bf16),
            pltpu.VMEM((4, 2, 2, SEQ // 2, 128), bf16),
            pltpu.VMEM((SEQ, 512), bf16),
            dma, dma((4,)), dma, dma((4, 5)), dma((4, 5)), dma((4, 2)), dma((24,)), dma, dma((6,)), dma, dma((4,)), dma((16,)),
        ],
        compiler_params=pltpu.CompilerParams(
            collective_id=0, has_side_effects=True, vmem_limit_bytes=VMEM_BYTES
        ),
        name="attend_project",
    )(span_start, span_len, queries, keys, values, out_weight.T)


def solution(mesh):
    placed = (P("dp", "mp"), P("dp", "mp"), P("dp", "mp"), P("mp", "dp"), P("dp"), P("dp"))
    return jax.shard_map(shards, mesh=mesh, in_specs=placed, out_specs=P("dp", "mp"), check_vma=False)
```

```python
import functools

import jax
import jax.numpy as jnp
from jax import lax
from jax.experimental import pallas as pl
from jax.experimental.pallas import tpu as pltpu
from jax.sharding import PartitionSpec as P

MESH = pl.DeviceIdType.MESH
HD = 128
BLK = 128
SEQ = 512
HEADS = 8
FEAT = HEADS * HD
NEG = -1e30
SCALE = 1.4426950408889634 / (128.0**0.5)
TRANS = (((1,), (1,)), ((), ()))
BEFORE, CUT1, CUT2 = 2, 5, 7
VMEM_BYTES = 53 << 20


def attend_head(q_ref, k_ref, v_ref, att, bias, h):
    cols = pl.ds(pl.multiple_of(h * HD, HD), HD)
    key = k_ref[:, cols]
    val = v_ref[:, cols]
    bounds = ((0, BLK, BLK), (BLK, 2 * BLK, SEQ), (2 * BLK, 3 * BLK, SEQ), (3 * BLK, SEQ, SEQ))
    scores = []
    for begin, end, keys in bounds:
        s = lax.dot_general(q_ref[begin:end, cols], key[:keys], TRANS, preferred_element_type=jnp.float32)
        scores.append(s + bias[begin:end, :keys])
    outs = []
    for s, (begin, end, keys) in zip(scores, bounds):
        top = jnp.max(s, axis=-1, keepdims=True)
        p = jnp.exp2((s - top) * SCALE)
        total = jnp.sum(p, axis=-1, keepdims=True)
        o = jnp.dot(p.astype(jnp.bfloat16), val[:keys], preferred_element_type=jnp.float32)
        outs.append((o / total).astype(jnp.bfloat16))
    for o, (begin, end, keys) in zip(outs, bounds):
        att[begin:end, cols] = o


def kernel(start_ref, len_ref, q_hbm, k_hbm, v_hbm, w_hbm, o_hbm,
           qkv, att, bias, wb, own, keep, xs, xm, xf, xr, out,
           osem, qsem, wsem, here_sem, y_sem, unit_sem, ws, fs, fr, xss, xrs, xms):
    dp, x = lax.axis_index("dp"), lax.axis_index("mp")
    c = lax.rem(dp, 2)
    y = lax.rem(lax.div(dp, 2), 4)
    z = lax.div(dp, 8)
    two = 2 - 4 * lax.rem(z, 2)

    def at(dz=0, dy=0, dx=0, dc=0):
        zz, yy = lax.rem(z + dz + 16, 16), lax.rem(y + dy + 4, 4)
        return ((zz * 4 + yy) * 2 + lax.rem(c + dc, 2), lax.rem(x + dx + 4, 4))

    def turn(a, r):
        return lax.rem(a + r + 4, 4)

    shift = (0, 1, -1, -two)
    zs = [lax.rem(z + d + 16, 16) for d in shift]
    a_of = [lax.div(zz, 4) for zz in zs]
    b_of = [lax.rem(zz, 4) for zz in zs]
    over_y = (1, -1, 2)
    near_z = (1, -1, two)
    lo, hi = pl.ds(0, FEAT // 2), pl.ds(FEAT // 2, FEAT // 2)

    barrier = pltpu.get_barrier_semaphore()
    partners = [at(dz=4), at(dz=-4), at(dz=1), at(dz=-1), at(dz=2), at(dz=-2),
                at(dy=1), at(dy=-1), at(dy=2), at(dx=1), at(dx=2), at(dx=3), at(dc=1)]
    for who in partners:
        pl.semaphore_signal(barrier, inc=1, device_id=who, device_id_type=MESH)

    w_in = pltpu.make_async_copy(w_hbm, wb.at[a_of[0], b_of[0], y, c], wsem)
    w_in.start()

    def quarter(i):
        return pl.ds(pl.multiple_of(i * 256, 256), 256)

    for i in range(4):
        for n, src in enumerate((q_hbm, k_hbm, v_hbm)):
            pltpu.make_async_copy(src.at[:, quarter(i)], qkv.at[n, :, quarter(i)], qsem.at[i]).start()

    row = lax.broadcasted_iota(jnp.int32, (SEQ, SEQ), 0)
    col = lax.broadcasted_iota(jnp.int32, (SEQ, SEQ), 1)
    first = start_ref[0] * BLK
    last = jnp.minimum(start_ref[0] + len_ref[0], SEQ // BLK) * BLK
    image_row = (row >= first) & (row < last)
    image_col = (col >= first) & (col < last)
    bias[...] = jnp.where(image_row, jnp.where(image_col, 0.0, NEG), jnp.where(col <= row, 0.0, NEG))

    def heads(from_head, to_head):
        def body(h, carry):
            @pl.when(lax.rem(h, 2) == 0)
            def _():
                i = lax.div(h, 2)
                pltpu.make_async_copy(qkv.at[:, :, quarter(i)], qkv.at[:, :, quarter(i)], qsem.at[i]).wait()

            attend_head(qkv.at[0], qkv.at[1], qkv.at[2], att, bias, h)
            return carry

        lax.fori_loop(from_head, to_head, body, 0)

    groups = []

    def send(ref, sem, whom, all_of):
        n = len(groups)
        for who in whom:
            pltpu.make_async_remote_copy(src_ref=ref, dst_ref=ref, send_sem=ws.at[n], recv_sem=sem,
                                         device_id=who, device_id_type=MESH).start()
        groups.append(all_of)

    def gone(n):
        pltpu.make_async_remote_copy(src_ref=groups[n], dst_ref=groups[n], send_sem=ws.at[n], recv_sem=ws.at[n],
                                     device_id=at(dc=1), device_id_type=MESH).wait_send()

    def got(ref, sem):
        pltpu.make_async_remote_copy(src_ref=ref, dst_ref=ref, send_sem=ws.at[0], recv_sem=sem,
                                     device_id=at(dc=1), device_id_type=MESH).wait_recv()

    every = pl.ds(0, FEAT)
    three = pl.ds(0, 3)
    kind = {(0, 0): (0, every), (1, 0): (1, every), (-1, 0): (2, every), (2, 0): (3, lo), (2, 1): (4, hi)}

    def piece(n, r, part=0):
        a, b = turn(a_of[n], r), b_of[n]
        sem, feats = kind[r, part]
        return wb.at[a, b, y, c, :, feats], sem, wb.at[a, b, three, c, :, feats]

    def to_y(n, r, part=0):
        ref, sem, size = piece(n, r, part)
        send(ref, y_sem.at[b_of[n], sem], [at(dy=dy) for dy in over_y], size)

    def to_z(n, r, part=0):
        ref, sem, size = piece(n, r, part)
        send(ref, here_sem.at[b_of[n], sem], [at(dz=dz) for dz in near_z], size)

    def got_here(n, r, part=0):
        ref, sem, _ = piece(n, r, part)
        got(ref, here_sem.at[b_of[n], sem])

    def got_y(n, r, part=0):
        _, sem, size = piece(n, r, part)
        got(size, y_sem.at[b_of[n], sem])

    def rest(n, r):
        sem, feats = (0, every) if r == 1 else (1, hi)
        a, b = turn(a_of[n], r), b_of[n]
        return a, b, feats, unit_sem.at[b, sem]

    def rest_to_z(r):
        a, b, feats, sem = rest(0, r)
        m = len(groups)
        for dy in over_y:
            ref = wb.at[a, b, turn(y, dy), c, :, feats]
            for dz in near_z:
                pltpu.make_async_remote_copy(src_ref=ref, dst_ref=ref, send_sem=ws.at[m], recv_sem=sem,
                                             device_id=at(dz=dz), device_id_type=MESH).start()
        groups.append(wb.at[three, b, three, c, :, feats])

    def got_rest(n, r):
        a, b, feats, sem = rest(n, r)
        got(wb.at[a, b, three, c, :, feats], sem)

    blocks = []

    def across(n, r, g):
        ref = wb.at[turn(a_of[n], r), b_of[n], :, c]
        pltpu.make_async_remote_copy(src_ref=ref, dst_ref=ref, send_sem=fs, recv_sem=fr.at[g],
                                     device_id=at(dc=1), device_id_type=MESH).start()
        blocks.append((n, r))

    half = SEQ // 2
    top, low_half = pl.ds(0, half), pl.ds(half, half)

    def hop(m, dst, rows, k, sem, to):
        return pltpu.make_async_remote_copy(src_ref=xs.at[m, rows], dst_ref=dst, send_sem=xss, recv_sem=sem,
                                            device_id=(dp, to), device_id_type=MESH)

    def to_dest(n, m, side, k):
        a = turn(a_of[n], blocks[m][1])
        rows = top if k == 0 else low_half
        return hop(m, xr.at[n, side, k], rows, k, xrs.at[n], a)

    def to_dest_f(n, m, side, k):
        a = turn(a_of[n], blocks[m][1])
        return pltpu.make_async_remote_copy(src_ref=xf.at[m], dst_ref=xr.at[n, side, k], send_sem=xss,
                                            recv_sem=xrs.at[n], device_id=(dp, a), device_id_type=MESH)

    def to_middle(m, k):
        rows = top if k == 0 else low_half
        return hop(m, xm.at[m], rows, k, xms.at[m], turn(x, -1 if k == 0 else 1))

    def project(g, *ms):
        got(wb.at[pl.ds(0, len(ms)), 0, :, 1 - c], fr.at[g])
        ws_in = []
        for m in ms:
            n, r = blocks[m]
            ws_in.append(wb[turn(a_of[n], r), b_of[n]].reshape(128, FEAT))
        w = ws_in[0] if len(ws_in) == 1 else jnp.concatenate(ws_in, axis=0)
        parts = lax.dot_general(att[...], w, TRANS, preferred_element_type=jnp.float32)
        for k, m in enumerate(ms):
            n, r = blocks[m]
            a = turn(a_of[n], r)
            part = parts[:, k * 128:(k + 1) * 128]

            away = turn(a, -x)

            @pl.when(away == 0)
            def _(n=n, part=part):
                own[n] = part

            @pl.when(away != 0)
            def _(m=m, part=part):
                xs[m] = part.astype(jnp.bfloat16)

            @pl.when(away == 1)
            def _(n=n, m=m, part=part):
                keep[m] = part[half:]
                to_dest(n, m, 1, 0).start()

            @pl.when(away == 3)
            def _(n=n, m=m, part=part):
                keep[m] = part[:half]
                to_dest(n, m, 0, 1).start()

            @pl.when(away == 2)
            def _(m=m):
                to_middle(m, 0).start()
                to_middle(m, 1).start()

    def forward(*ms):
        for m in ms:
            n, r = blocks[m]
            away = turn(turn(a_of[n], r), -x)
            for here, side, k in ((1, 1, 1), (3, 0, 0)):
                @pl.when(away == here)
                def _(n=n, m=m, side=side, k=k):
                    got(xm.at[m], xms.at[m])
                    rows = top if k == 0 else low_half
                    fs_m = (keep[m] + xm[m].astype(jnp.float32)).astype(jnp.bfloat16)
                    xf[m] = fs_m
                    to_dest_f(n, m, side, k).start()

    heads(0, BEFORE)
    w_in.wait()
    pl.semaphore_wait(barrier, len(partners))
    to_z(0, 0)
    mine = wb.at[a_of[0], b_of[0], y, c]
    n_out = len(groups)
    for dz, sem in ((4, 2), (-4, 1)):
        pltpu.make_async_remote_copy(src_ref=mine, dst_ref=mine, send_sem=ws.at[n_out],
                                     recv_sem=here_sem.at[b_of[0], sem],
                                     device_id=at(dz=dz), device_id_type=MESH).start()
    groups.append(wb.at[a_of[0], b_of[0], pl.ds(0, 2), c])
    to_y(0, 0)
    heads(BEFORE, CUT1)
    for n in (1, 2, 3):
        got_here(n, 0)
        to_y(n, 0)
    heads(CUT1, CUT2)
    got_here(0, 1)
    got_here(0, -1)
    n_out = len(groups)
    for r, dz, feats, sem in ((-1, 4, lo, 3), (1, -4, hi, 4)):
        ref = wb.at[turn(a_of[0], r), b_of[0], y, c, :, feats]
        pltpu.make_async_remote_copy(src_ref=ref, dst_ref=ref, send_sem=ws.at[n_out],
                                     recv_sem=here_sem.at[b_of[0], sem],
                                     device_id=at(dz=dz), device_id_type=MESH).start()
    groups.append(wb.at[a_of[0], b_of[0], y, c])
    to_y(0, 1)
    to_z(0, 1)
    to_y(0, -1)
    to_z(0, -1)
    got_y(0, 0)
    across(0, 0, 0)
    heads(CUT2, HEADS)
    for n in (1, 2, 3):
        got_y(n, 0)
        across(n, 0, 1)
    project(0, 0)
    got_y(0, 1)
    across(0, 1, 1)
    got_here(0, 2)
    to_z(0, 2)
    to_y(0, 2)
    got_here(0, 2, 1)
    to_z(0, 2, 1)
    to_y(0, 2, 1)
    rest_to_z(1)
    for n in (1, 2, 3):
        got_here(n, -1)
        to_y(n, -1)
    got_y(0, -1)
    across(0, -1, 2)
    project(1, 1, 2, 3, 4)
    forward(0)
    for n in (1, 2, 3):
        got_here(n, 2)
        to_y(n, 2)
    project(2, 5)
    got_y(0, 2, 1)
    rest_to_z(2)
    got_y(0, 2)
    across(0, 2, 3)
    for n in (1, 2, 3):
        got_here(n, 1)
        got_rest(n, 1)
        across(n, 1, 3)
    for n in (1, 2, 3):
        got_y(n, -1)
        across(n, -1, 4)
    forward(1, 2)
    project(3, 6, 7, 8, 9)
    project(4, 10, 11, 12)
    forward(3, 4, 5)
    for n in (1, 2, 3):
        got_here(n, 2, 1)
        got_rest(n, 2)
        got_y(n, 2)
        across(n, 2, 5)
    project(5, 13, 14, 15)
    for m in range(6, 16):
        forward(m)
        if m > 8:
            for n in range(3 * m - 27, 3 * m - 24):
                gone(n)
    for n in range(21, len(groups)):
        gone(n)
    for n in range(4):
        cols = pl.ds(pl.multiple_of(b_of[n] * 128, 128), 128)
        got(xr.at[n], xrs.at[n])
        for k, rows in ((0, top), (1, low_half)):
            total = own[n, rows]
            for side in range(2):
                total = total + xr[n, side, k].astype(jnp.float32)
            out[rows, cols] = total.astype(jnp.bfloat16)
        pltpu.make_async_copy(out.at[:, cols], o_hbm.at[:, cols], osem).start()
    both = wb.at[:, :, :, c]
    pltpu.make_async_remote_copy(src_ref=both, dst_ref=both, send_sem=fs, recv_sem=fs,
                                 device_id=at(dc=1), device_id_type=MESH).wait_send()
    most = xs.at[pl.ds(0, 12)]
    pltpu.make_async_remote_copy(src_ref=most, dst_ref=most, send_sem=xss, recv_sem=xss,
                                 device_id=at(dc=1), device_id_type=MESH).wait_send()
    pltpu.make_async_copy(out, o_hbm, osem).wait()


def shards(queries, keys, values, out_weight, span_start, span_len):
    hbm = pl.BlockSpec(memory_space=pltpu.HBM)
    smem = pl.BlockSpec(memory_space=pltpu.SMEM)
    bf16, f32 = jnp.bfloat16, jnp.float32
    dma = pltpu.SemaphoreType.DMA
    return pl.pallas_call(
        kernel,
        out_shape=jax.ShapeDtypeStruct((SEQ, 512), bf16),
        in_specs=[smem, smem, hbm, hbm, hbm, hbm],
        out_specs=pl.BlockSpec(memory_space=pl.ANY),
        scratch_shapes=[
            pltpu.VMEM((3, SEQ, FEAT), bf16),
            pltpu.VMEM((SEQ, FEAT), bf16),
            pltpu.VMEM((SEQ, SEQ), f32),
            pltpu.VMEM((4, 4, 4, 2, 16, FEAT), bf16),
            pltpu.VMEM((4, SEQ, 128), f32),
            pltpu.VMEM((16, SEQ // 2, 128), f32),
            pltpu.VMEM((16, SEQ, 128), bf16),
            pltpu.VMEM((16, SEQ // 2, 128), bf16),
            pltpu.VMEM((16, SEQ // 2, 128), bf16),
            pltpu.VMEM((4, 2, 2, SEQ // 2, 128), bf16),
            pltpu.VMEM((SEQ, 512), bf16),
            dma, dma((4,)), dma, dma((4, 5)), dma((4, 5)), dma((4, 2)), dma((24,)), dma, dma((6,)), dma, dma((4,)), dma((16,)),
        ],
        compiler_params=pltpu.CompilerParams(
            collective_id=0, has_side_effects=True, vmem_limit_bytes=VMEM_BYTES
        ),
        name="attend_project",
    )(span_start, span_len, queries, keys, values, out_weight.T)


def solution(mesh):
    placed = (P("dp", "mp"), P("dp", "mp"), P("dp", "mp"), P("mp", "dp"), P("dp"), P("dp"))
    return jax.shard_map(shards, mesh=mesh, in_specs=placed, out_specs=P("dp", "mp"), check_vma=False)
```
